1024 devices in a mesh: slab: 512 (over z, y, x), bal: 2 (over core).
Axes of the slice: x: 8, y: 8, z: 8, core: 2. Of those that a mesh axis runs over, the one named last changes fastest.
Arguments:
- order_parameter: float32 [512, 4, 32, 1024], P('slab', 'bal'), may hold values from -1 to 1
- concentration_excess: float32 [512, 4, 32, 1024], P('slab', 'bal'), may hold values from -1.8 to 1.8
- thermal_subcooling: float32 [512, 4, 32, 1024], P('slab', 'bal'), may hold values from -1.8 to 1.8
- holder_places_prior: int32 [512, 4], replicated, may hold values from 0 to 3, as said below
- holder_places_revised: int32 [512, 4], replicated, may hold values from 0 to 3, as said below
- update_flags: int32 [512, 4], replicated, may hold values 0 or 1
Outputs:
- phase_out: float32 [512, 4, 32, 1024], P('slab', 'bal')
- solute_out: float32 [512, 4, 32, 1024], P('slab', 'bal')
- temperature_out: float32 [512, 4, 32, 1024], P('slab', 'bal')
The draws below stay inside these ranges and needn't reach their ends.
Inputs may be any that keep to these rules, and one draw needn't show every extreme that they name: `holder_places_prior`: each row is a permutation of the 4 positions of a layer; slot k belongs to the owner of index k // 2 along bal. `holder_places_revised`: each row is a permutation of the layer's positions. In every layer each owner gives exactly 1 of its blocks to other owners and receives exactly 1; every other block keeps its slot.
All inputs are finite; a program needn't handle non-finite values.
Results may differ from the reference program's by a relative error of at most 0.00002.
Values sent between devices are 32-bit elements; how exact they have to be, the bound alone decides.
A program may use at most 32 MiB of HBM per device.

```python
import jax
import jax.numpy as jnp

TILE_SIDE_POINTS = 32
BZ = 4
BLK_DEV = 2
STEPS = 1
SHEET_COUNT = 512
TILES_IN_SHEET = 4
BY = 1
MOVE = 1


def small_permutation(sub_key):
    return jax.random.permutation(sub_key, BLK_DEV)


def layer_slots(layer_key):
    devices = TILES_IN_SHEET // BLK_DEV
    key_perm, key_rank, key_cycle = jax.random.split(layer_key, 3)
    before = jax.random.permutation(key_perm, TILES_IN_SHEET).astype(jnp.int32)
    ranks = jax.vmap(small_permutation)(jax.random.split(key_rank, devices))
    slot_of_rank = jnp.argsort(ranks, axis=1).astype(jnp.int32)
    after = before
    cycle_keys = jax.random.split(key_cycle, MOVE)
    for turn in range(MOVE):
        order = jax.random.permutation(cycle_keys[turn], devices).astype(jnp.int32)
        place = jnp.argsort(order).astype(jnp.int32)
        target = order[(place + 1) % devices]
        source_slots = jnp.arange(devices, dtype=jnp.int32) * BLK_DEV + slot_of_rank[:, turn]
        target_slots = target * BLK_DEV + slot_of_rank[target, turn]
        after = after.at[target_slots].set(before[source_slots])
    return (before, after)


def shared_slots(key):
    base = jax.random.fold_in(key, 7)
    return jax.vmap(layer_slots)(jax.random.split(base, SHEET_COUNT))


def draw_holder_places_prior(key, part):
    return shared_slots(key)[0]


def draw_holder_places_revised(key, part):
    return shared_slots(key)[1]


def set_ends(array, key, smallest, largest):
    longest = array.shape.index(max(array.shape))
    spots = []
    for shift in (0, 1):
        where = [jax.random.randint(jax.random.fold_in(key, axis), (), 0, length) for axis, length in enumerate(array.shape)]
        where[longest] = (where[longest] + shift) % array.shape[longest]
        spots.append(tuple(where))
    return array.at[spots[0]].set(smallest).at[spots[1]].set(largest)


def block_scale(rng, extent, pieces, low, top_value):
    level = 1.0
    for dim, parts in pieces:
        steps = jax.random.uniform(jax.random.fold_in(jax.random.fold_in(rng, 6), dim), (parts,), jnp.float32, low / len(pieces), top_value / len(pieces))
        level = level * jnp.repeat(jnp.exp(steps), extent[dim] // parts).reshape((-1,) + (1,) * (len(extent) - 1 - dim))
    return level


def bell_draw(stream_key, extent, width, most, pieces=(), kind=jnp.bfloat16):
    loudness = block_scale(stream_key, extent, pieces, -0.22, 0.18) if pieces else 1.0
    entries = jax.random.normal(stream_key, extent, jnp.float32) * width * loudness
    return jnp.minimum(jnp.maximum(entries, -most), most).astype(kind)


def setup_inputs(seed: int = 0) -> dict:
    key_list = jax.random.split(jax.random.key(seed), 7)
    return {
        "order_parameter": jnp.clip(jax.random.uniform(key_list[0], (SHEET_COUNT, TILES_IN_SHEET, TILE_SIDE_POINTS, TILE_SIDE_POINTS * TILE_SIDE_POINTS), jnp.float32, -1.0, 1.0) * block_scale(key_list[0], (SHEET_COUNT, TILES_IN_SHEET, TILE_SIDE_POINTS, TILE_SIDE_POINTS * TILE_SIDE_POINTS), ((0, 512), (1, 2)), -0.4, 0.0), -1.0, 1.0),
        "concentration_excess": bell_draw(key_list[1], (SHEET_COUNT, TILES_IN_SHEET, TILE_SIDE_POINTS, TILE_SIDE_POINTS * TILE_SIDE_POINTS), 0.3, 1.8, ((0, 512), (1, 2)), jnp.float32),
        "thermal_subcooling": bell_draw(key_list[2], (SHEET_COUNT, TILES_IN_SHEET, TILE_SIDE_POINTS, TILE_SIDE_POINTS * TILE_SIDE_POINTS), 0.3, 1.8, ((0, 512), (1, 2)), jnp.float32),
        "holder_places_prior": draw_holder_places_prior(jax.random.fold_in(key_list[6], 71), 0),
        "holder_places_revised": draw_holder_places_revised(jax.random.fold_in(key_list[6], 71), 0),
        "update_flags": set_ends((jax.random.randint(key_list[5], (SHEET_COUNT, TILES_IN_SHEET), 0, 4) < 3).astype(jnp.int32), jax.random.fold_in(key_list[5], 1), 0, 1),
    }


RATE = 0.1
ANISO = 0.05
COUPLE = 0.5
DIFF_SOLUTE = 0.08
DIFF_HEAT = 0.15
TINY = 1e-4


def laplace(center, neighbours):
    return ((neighbours[0] + neighbours[1]) + (neighbours[2] + neighbours[3])) + (neighbours[4] + neighbours[5]) - 6.0 * center


def march_forward(phase_now, solute_now, heat_now, near_phase, near_solute, near_heat, active_now):
    slope_x = 0.5 * (near_phase[0] - near_phase[1])
    slope_y = 0.5 * (near_phase[2] - near_phase[3])
    slope_z = 0.5 * (near_phase[4] - near_phase[5])
    sq_x = slope_x * slope_x
    sq_y = slope_y * slope_y
    sq_z = slope_z * slope_z
    slope_sq = sq_x + sq_y + sq_z
    quartic = sq_x * sq_x + sq_y * sq_y + sq_z * sq_z
    fourth_ratio = quartic / (slope_sq * slope_sq + TINY)
    anisotropy = (1.0 - 3.0 * ANISO) + 4.0 * ANISO * fourth_ratio
    well_term = 1.0 - phase_now * phase_now
    forcing = phase_now - phase_now * phase_now * phase_now - COUPLE * well_term * well_term * (solute_now + heat_now)
    phase_new = phase_now + active_now * (RATE * (anisotropy * anisotropy * laplace(phase_now, near_phase) + forcing))
    change = phase_new - phase_now
    solute_new = solute_now + DIFF_SOLUTE * laplace(solute_now, near_solute) + 0.5 * change
    heat_new = heat_now + DIFF_HEAT * laplace(heat_now, near_heat) + 0.5 * change
    return phase_new, solute_new, heat_new


def mesh_adjacent(grid):
    x_upper = jnp.concatenate([grid[1:], grid[-1:]], axis=0)
    x_lower = jnp.concatenate([grid[:1], grid[:-1]], axis=0)
    y_upper = jnp.roll(grid, -1, axis=1)
    y_lower = jnp.roll(grid, 1, axis=1)
    z_upper = jnp.roll(grid, -1, axis=2)
    z_lower = jnp.roll(grid, 1, axis=2)
    return (x_upper, x_lower, y_upper, y_lower, z_upper, z_lower)


def arrange_as_mesh(blocks, slots):
    inverse = jnp.argsort(slots, axis=1).astype(jnp.int32)
    placed = jnp.take_along_axis(blocks, inverse[:, :, None, None], axis=1)
    placed = placed.reshape(SHEET_COUNT, BY, BZ, TILE_SIDE_POINTS, TILE_SIDE_POINTS, TILE_SIDE_POINTS)
    return placed.transpose(0, 3, 1, 4, 2, 5).reshape(SHEET_COUNT * TILE_SIDE_POINTS, BY * TILE_SIDE_POINTS, BZ * TILE_SIDE_POINTS)


def unpack_mesh(grid, slots):
    placed = grid.reshape(SHEET_COUNT, TILE_SIDE_POINTS, BY, TILE_SIDE_POINTS, BZ, TILE_SIDE_POINTS).transpose(0, 2, 4, 1, 3, 5)
    placed = placed.reshape(SHEET_COUNT, TILES_IN_SHEET, TILE_SIDE_POINTS, TILE_SIDE_POINTS * TILE_SIDE_POINTS)
    return jnp.take_along_axis(placed, slots.astype(jnp.int32)[:, :, None, None], axis=1)


def reference(order_parameter, concentration_excess, thermal_subcooling, holder_places_prior, holder_places_revised, update_flags):
    order_parameter_mesh = arrange_as_mesh(order_parameter, holder_places_prior)
    concentration_mesh = arrange_as_mesh(concentration_excess, holder_places_prior)
    thermal_mesh = arrange_as_mesh(thermal_subcooling, holder_places_prior)
    update_flags_mesh = update_flags.astype(jnp.float32).reshape(SHEET_COUNT, 1, BY, 1, BZ, 1)
    update_flags_mesh = jnp.broadcast_to(update_flags_mesh, (SHEET_COUNT, TILE_SIDE_POINTS, BY, TILE_SIDE_POINTS, BZ, TILE_SIDE_POINTS)).reshape(SHEET_COUNT * TILE_SIDE_POINTS, BY * TILE_SIDE_POINTS, BZ * TILE_SIDE_POINTS)
    for sweep_index in range(2 * STEPS):
        order_parameter_mesh, concentration_mesh, thermal_mesh = march_forward(order_parameter_mesh, concentration_mesh, thermal_mesh, mesh_adjacent(order_parameter_mesh), mesh_adjacent(concentration_mesh), mesh_adjacent(thermal_mesh), update_flags_mesh)
    return (unpack_mesh(order_parameter_mesh, holder_places_revised), unpack_mesh(concentration_mesh, holder_places_revised), unpack_mesh(thermal_mesh, holder_places_revised))
```

```python
import functools

import jax
import jax.numpy as jnp
from jax import lax
from jax.experimental import pallas as pl
from jax.experimental.pallas import tpu as pltpu
from jax.sharding import PartitionSpec as P

RATE = 0.1
ANISO = 0.05
COUPLE = 0.5
DIFF_SOLUTE = 0.08
DIFF_HEAT = 0.15
TINY = 0.0001

MESH = pl.DeviceIdType.MESH
F32 = jnp.float32


def chunk_swap(planes, lane_block):
    turned = [planes[0]] + [pltpu.roll(planes[p], 32 * p, 1) for p in (1, 2, 3)]
    out = []
    for k in range(4):
        pick = [turned[(j - k) % 4] for j in range(4)]
        low = jnp.where(lane_block[0], pick[0], pick[1])
        high = jnp.where(lane_block[2], pick[2], pick[3])
        both = jnp.where(lane_block[1], low, high)
        out.append(both if k == 0 else pltpu.roll(both, 128 - 32 * k, 1))
    return out


def advance(center, below, above, active):
    def near(f, r):
        plane = center[f]
        y_upper = plane[r + 1] if r < 3 else pltpu.roll(plane[0], 7, 0)
        y_lower = plane[r - 1] if r > 0 else pltpu.roll(plane[3], 1, 0)
        z_upper = pltpu.roll(plane[r], 127, 1)
        z_lower = pltpu.roll(plane[r], 1, 1)
        return above[f][r], below[f][r], y_upper, y_lower, z_upper, z_lower

    def total(n):
        return ((n[0] + n[1]) + (n[2] + n[3])) + (n[4] + n[5])

    out = [[], [], []]
    for r in range(4):
        phase, solute, heat = center[0][r], center[1][r], center[2][r]
        n = near(0, r)
        dx, dy, dz = n[0] - n[1], n[2] - n[3], n[4] - n[5]
        qx, qy, qz = dx * dx, dy * dy, dz * dz
        slope_sq = qx + qy + qz
        quartic = qx * qx + qy * qy + qz * qz
        ratio = quartic / (slope_sq * slope_sq + 16.0 * TINY)
        aniso = (1.0 - 3.0 * ANISO) + 4.0 * ANISO * ratio
        well = 1.0 - phase * phase
        forcing = phase * well - (COUPLE * (well * well)) * (solute + heat)
        change = active * (aniso * aniso * (total(n) - 6.0 * phase) + forcing)
        half = 0.5 * change
        out[0].append(phase + change)
        out[1].append(solute + DIFF_SOLUTE * (total(near(1, r)) - 6.0 * solute) + half)
        out[2].append(heat + DIFF_HEAT * (total(near(2, r)) - 6.0 * heat) + half)
    return out


def kernel(
    slabs,
    p_in,
    u_in,
    h_in,
    prior_in,
    revised_in,
    flags_in,
    p_out,
    u_out,
    h_out,
    main,
    extra,
    halo,
    first,
    second,
    final,
    leaving,
    prior,
    revised,
    flags,
    table_sem,
    local_sem,
    chip_send,
    chip_recv,
    side_send,
    side_recv,
    back_send,
    back_recv,
):
    fields = (p_in, u_in, h_in)
    outs = (p_out, u_out, h_out)
    s = lax.axis_index("slab")
    b = lax.axis_index("bal")
    ob = 1 - b
    last = slabs - 1
    has_low, has_high = s > 0, s < last
    barrier = pltpu.get_barrier_semaphore()

    pl.semaphore_signal(barrier, inc=1, device_id=(s, ob), device_id_type=MESH)

    @pl.when((b == 0) & has_low)
    def _():
        for k in range(2):
            pl.semaphore_signal(barrier, inc=1, device_id=(s - 1, k), device_id_type=MESH)

    @pl.when((b == 1) & has_high)
    def _():
        for k in range(2):
            pl.semaphore_signal(barrier, inc=1, device_id=(s + 1, k), device_id_type=MESH)

    tables = [
        pltpu.make_async_copy(src, dst, table_sem.at[i])
        for i, (src, dst) in enumerate(
            ((prior_in, prior), (revised_in, revised), (flags_in, flags))
        )
    ]
    for t in tables:
        t.start()
    pl.semaphore_wait(barrier, 1 + jnp.where(has_low, 1, 0) + jnp.where(has_high, 1, 0))

    def other_core(src, dst, i):
        return pltpu.make_async_remote_copy(
            src, dst, chip_send.at[i], chip_recv.at[i], device_id=(s, ob), device_id_type=MESH
        )

    mine = pl.ds(2 * b, 2)
    theirs = pl.ds(2 * ob, 2)

    def edge_row(core, j):
        return 2 - core, jnp.where(core == 1, 6 + j, 1 - j)

    for f in range(3):
        for j in range(2):
            t, i = edge_row(ob, j)
            other_core(fields[f].at[:, t, :, i], extra.at[f, j, mine], 1).start()
        for c in range(8):
            other_core(fields[f].at[:, theirs, c], main.at[f, mine, :, :, c], 0).start()

    def to_layer(side, target):
        for f in range(3):
            for j in range(2):
                src = fields[f].at[:, 3, :, 7 - j] if side == 0 else fields[f].at[:, 0, :, j]
                pltpu.make_async_remote_copy(
                    src,
                    halo.at[b, f, j],
                    side_send.at[side],
                    side_recv,
                    device_id=(target, side),
                    device_id_type=MESH,
                ).start()

    @pl.when(has_high)
    def _():
        to_layer(0, s + 1)

    @pl.when(has_low)
    def _():
        to_layer(1, s - 1)

    for f in range(3):
        for j in range(2):
            t, i = edge_row(b, j)
            pltpu.make_async_copy(
                fields[f].at[:, t, :, i], extra.at[f, j, mine], local_sem.at[1]
            ).start()
        for c in range(8):
            pltpu.make_async_copy(
                fields[f].at[:, mine, c], main.at[f, mine, :, :, c], local_sem.at[0]
            ).start()

    for t in tables:
        t.wait()
    next_to = jnp.where(b == 0, jnp.where(has_low, s - 1, s), jnp.where(has_high, s + 1, s))
    at_wall = ((b == 0) & (s == 0)) | ((b == 1) & (s == last))

    def slots_of(table, row):
        held = [table[k, row] for k in range(4)]
        return [
            jnp.where(held[1] == p, 1, jnp.where(held[2] == p, 2, jnp.where(held[3] == p, 3, 0)))
            for p in range(4)
        ]

    slot_here = slots_of(prior, s)
    slot_next = slots_of(prior, next_to)
    place_mine = [revised[2 * b + k, s] for k in range(2)]
    place_theirs = [revised[2 * ob + k, s] for k in range(2)]
    lane = lax.broadcasted_iota(jnp.int32, (8, 128), 1)
    lane_block = [lane < 32, lane < 64, lane < 96]

    def activity(row):
        a = [RATE * flags[p, row].astype(F32) for p in range(4)]
        low = jnp.where(lane_block[0], a[0], a[1])
        high = jnp.where(lane_block[2], a[2], a[3])
        return jnp.where(lane_block[1], low, high)

    active_here = activity(s)
    active_next = activity(next_to)

    def row_of(u):
        return jnp.where(b == 1, u - 2, 17 - u)

    def keep(u, planes, f):
        for r in range(4):
            first[f, u, r] = planes[r]

    def gather_extra(j):
        for f in range(3):
            keep(j, chunk_swap([extra[f, j, slot_here[p]] for p in range(4)], lane_block), f)

    def gather(u):
        row = row_of(u)
        for f in range(3):
            planes = [main[f, slot_here[p], row // 8, row % 8] for p in range(4)]
            keep(u, chunk_swap(planes, lane_block), f)

    def gather_halo(j):
        for f in range(3):
            planes = chunk_swap(
                [halo[slot_next[p] // 2, f, j, slot_next[p] % 2] for p in range(4)], lane_block
            )
            keep(18 + j, [jnp.where(at_wall, first[f, 17, r], planes[r]) for r in range(4)], f)

    def rows(src, u):
        return [[src[f, u, r] for r in range(4)] for f in range(3)]

    def step_one(u, active):
        new = advance(rows(first, u), rows(first, u - 1), rows(first, u + 1), active)
        for f in range(3):
            for r in range(4):
                second[f, u, r] = new[f][r]
        return new

    def step_two(u):
        new = advance(rows(second, u), rows(second, u - 1), rows(second, u + 1), active_here)
        for f in range(3):
            planes = chunk_swap(new[f], lane_block)
            for p in range(4):
                final[f, p, u - 2] = planes[p]

    def deal(u):
        row = row_of(u)
        for f in range(3):
            for k in range(2):
                leaving[f, k, row // 8, row % 8] = final[f, place_theirs[k], u - 2]
                outs[f][k, 2 * b + row // 8, row % 8] = final[f, place_mine[k], u - 2]

    pltpu.make_async_copy(main.at[:, mine], main.at[:, mine], local_sem.at[0]).wait()
    pltpu.make_async_copy(extra.at[:, :, mine], extra.at[:, :, mine], local_sem.at[1]).wait()
    other_core(main.at[:, mine], main.at[:, theirs], 0).wait_recv()
    other_core(extra.at[:, :, mine], extra.at[:, :, theirs], 1).wait_recv()

    gather_extra(0)
    gather_extra(1)
    gather(2)
    step_one(1, active_here)
    gather(3)
    step_one(2, active_here)
    gather(4)
    step_one(3, active_here)
    gather(5)

    def stage(t, carry):
        step_two(t - 4)
        step_one(t - 2, active_here)
        gather(t)
        return carry

    lax.fori_loop(6, 18, stage, 0)
    step_two(14)
    step_one(16, active_here)
    step_two(15)

    def side_copy(side, ref):
        return pltpu.make_async_remote_copy(
            ref, ref, side_send.at[side], side_recv, device_id=(s, ob), device_id_type=MESH
        )

    @pl.when(jnp.logical_not(at_wall))
    def _():
        side_copy(0, halo).wait_recv()

    gather_halo(0)
    gather_halo(1)
    step_one(17, active_here)
    beside = step_one(18, active_next)
    for f in range(3):
        for r in range(4):
            second[f, 18, r] = jnp.where(at_wall, second[f, 17, r], beside[f][r])
    step_two(16)
    step_two(17)

    def deal_all(t, carry):
        for i in range(4):
            deal(2 + 4 * t + i)
        return carry

    lax.fori_loop(0, 4, deal_all, 0)

    def back(f):
        return pltpu.make_async_remote_copy(
            leaving.at[f],
            outs[f].at[:, pl.ds(2 * b, 2)],
            back_send.at[f],
            back_recv.at[f],
            device_id=(s, ob),
            device_id_type=MESH,
        )

    for f in range(3):
        back(f).start()
    other_core(main.at[:, mine], main.at[:, theirs], 0).wait_send()
    other_core(extra.at[:, :, mine], extra.at[:, :, theirs], 1).wait_send()

    @pl.when(has_high)
    def _():
        side_copy(0, halo.at[b]).wait_send()

    @pl.when(has_low)
    def _():
        side_copy(1, halo.at[b]).wait_send()

    for f in range(3):
        back(f).wait()


def deliver(p_in, u_in, h_in, p_out, u_out, h_out, sem):
    copies = []
    for f, (src, dst) in enumerate(((p_in, p_out), (u_in, u_out), (h_in, h_out))):
        for c in range(8):
            copies.append(
                pltpu.make_async_copy(src.at[:, :, :, c], dst.at[:, :, c], sem.at[f, c])
            )
    for copy in copies:
        copy.start()
    for copy in copies:
        copy.wait()


def body(slabs, p, u, h, prior, revised, flags):
    tiles = [a.reshape(2, 4, 8, 8, 128).transpose(0, 1, 3, 2, 4) for a in (p, u, h)]
    block = jax.ShapeDtypeStruct((2, 4, 8, 8, 128), F32)
    anywhere = pl.BlockSpec(memory_space=pl.ANY)
    hbm = pl.BlockSpec(memory_space=pltpu.HBM)
    vmem = pl.BlockSpec(memory_space=pltpu.VMEM)
    dma = pltpu.SemaphoreType.DMA
    table = pltpu.SMEM((4, slabs), jnp.int32)
    done = pl.pallas_call(
        functools.partial(kernel, slabs),
        out_shape=(block,) * 3,
        in_specs=[hbm] * 6,
        out_specs=(vmem,) * 3,
        scratch_shapes=[
            pltpu.VMEM((3, 4, 2, 8, 8, 128), F32),
            pltpu.VMEM((3, 2, 4, 8, 128), F32),
            pltpu.VMEM((2, 3, 2, 2, 8, 128), F32),
            pltpu.VMEM((3, 20, 4, 8, 128), F32),
            pltpu.VMEM((3, 20, 4, 8, 128), F32),
            pltpu.VMEM((3, 4, 16, 8, 128), F32),
            pltpu.VMEM((3, 2, 2, 8, 8, 128), F32),
            table,
            table,
            table,
            dma((3,)),
            dma((2,)),
            dma((2,)),
            dma((2,)),
            dma((2,)),
            dma,
            dma((3,)),
            dma((3,)),
        ],
        compiler_params=pltpu.CompilerParams(
            collective_id=0, has_side_effects=True, vmem_limit_bytes=16 << 20
        ),
        name="sweeps",
    )(*(pltpu.with_memory_space_constraint(a, pltpu.HBM) for a in (*tiles, prior.T, revised.T, flags.T)))
    placed = pl.pallas_call(
        deliver,
        out_shape=(block,) * 3,
        in_specs=[anywhere] * 3,
        out_specs=(anywhere,) * 3,
        scratch_shapes=[dma((3, 8))],
        compiler_params=pltpu.CompilerParams(vmem_limit_bytes=4 << 20),
        name="deliver",
    )(*done)
    return tuple(a.transpose(0, 1, 3, 2, 4).reshape(1, 2, 32, 1024) for a in placed)


def solution(mesh):
    blocks = P("slab", "bal", None, None)
    return jax.shard_map(
        functools.partial(body, mesh.shape["slab"]),
        mesh=mesh,
        in_specs=(blocks,) * 3 + (P(),) * 3,
        out_specs=(blocks,) * 3,
        check_vma=False,
    )
```

```python
import functools

import jax
import jax.numpy as jnp
from jax import lax
from jax.experimental import pallas as pl
from jax.experimental.pallas import tpu as pltpu
from jax.sharding import PartitionSpec as P

RATE = 0.1
ANISO = 0.05
COUPLE = 0.5
DIFF_SOLUTE = 0.08
DIFF_HEAT = 0.15
TINY = 0.0001

MESH = pl.DeviceIdType.MESH
F32 = jnp.float32


def chunk_swap(planes, lane_block):
    turned = [planes[0]] + [pltpu.roll(planes[p], 32 * p, 1) for p in (1, 2, 3)]
    out = []
    for k in range(4):
        pick = [turned[(j - k) % 4] for j in range(4)]
        low = jnp.where(lane_block[0], pick[0], pick[1])
        high = jnp.where(lane_block[2], pick[2], pick[3])
        both = jnp.where(lane_block[1], low, high)
        out.append(both if k == 0 else pltpu.roll(both, 128 - 32 * k, 1))
    return out


def advance(center, below, above, active):
    def total(f, r):
        plane = center[f]
        y_upper = plane[r + 1] if r < 3 else pltpu.roll(plane[0], 7, 0)
        y_lower = plane[r - 1] if r > 0 else pltpu.roll(plane[3], 1, 0)
        z_upper, z_lower = pltpu.roll(plane[r], 127, 1), pltpu.roll(plane[r], 1, 1)
        around = ((above[f][r] + below[f][r]) + (y_upper + y_lower)) + (z_upper + z_lower)
        return around, y_upper - y_lower, z_upper - z_lower

    out = [[], [], []]
    for r in range(4):
        phase, solute, heat = center[0][r], center[1][r], center[2][r]
        around, dy, dz = total(0, r)
        dx = above[0][r] - below[0][r]
        qx, qy, qz = dx * dx, dy * dy, dz * dz
        slope_sq = qx + qy + qz
        quartic = qx * qx + qy * qy + qz * qz
        ratio = quartic / (slope_sq * slope_sq + 16.0 * TINY)
        aniso = (1.0 - 3.0 * ANISO) + 4.0 * ANISO * ratio
        well = 1.0 - phase * phase
        forcing = well * (phase - (COUPLE * well) * (solute + heat))
        change = active * (aniso * aniso * (around - 6.0 * phase) + forcing)
        half = 0.5 * change
        out[0].append(phase + change)
        for f, rate, here in ((1, DIFF_SOLUTE, solute), (2, DIFF_HEAT, heat)):
            out[f].append(((1.0 - 6.0 * rate) * here + rate * total(f, r)[0]) + half)
    return out


def kernel(
    slabs,
    p_in,
    u_in,
    h_in,
    prior_in,
    revised_in,
    flags_in,
    p_out,
    u_out,
    h_out,
    main,
    extra,
    halo,
    first,
    second,
    final,
    leaving,
    prior,
    revised,
    flags,
    table_sem,
    local_sem,
    chip_send,
    chip_recv,
    side_send,
    side_recv,
    back_send,
    back_recv,
):
    fields = (p_in, u_in, h_in)
    outs = (p_out, u_out, h_out)
    s = lax.axis_index("slab")
    b = lax.axis_index("bal")
    ob = 1 - b
    last = slabs - 1
    has_low, has_high = s > 0, s < last
    barrier = pltpu.get_barrier_semaphore()

    pl.semaphore_signal(barrier, inc=1, device_id=(s, ob), device_id_type=MESH)

    @pl.when((b == 0) & has_low)
    def _():
        for k in range(2):
            pl.semaphore_signal(barrier, inc=1, device_id=(s - 1, k), device_id_type=MESH)

    @pl.when((b == 1) & has_high)
    def _():
        for k in range(2):
            pl.semaphore_signal(barrier, inc=1, device_id=(s + 1, k), device_id_type=MESH)

    tables = [
        pltpu.make_async_copy(src, dst, table_sem.at[i])
        for i, (src, dst) in enumerate(
            ((prior_in, prior), (revised_in, revised), (flags_in, flags))
        )
    ]
    for t in tables:
        t.start()
    pl.semaphore_wait(barrier, 1 + jnp.where(has_low, 1, 0) + jnp.where(has_high, 1, 0))

    def other_core(src, dst, i):
        return pltpu.make_async_remote_copy(
            src, dst, chip_send.at[i], chip_recv.at[i], device_id=(s, ob), device_id_type=MESH
        )

    mine = pl.ds(2 * b, 2)
    theirs = pl.ds(2 * ob, 2)

    def edge_row(core, j):
        return 2 - core, jnp.where(core == 1, 6 + j, 1 - j)

    for f in range(3):
        for j in range(2):
            t, i = edge_row(ob, j)
            other_core(fields[f].at[:, t, :, i], extra.at[f, j, mine], 1).start()
        for c in range(8):
            other_core(fields[f].at[:, theirs, c], main.at[f, mine, :, :, c], 0).start()

    def to_layer(side, target):
        for f in range(3):
            for j in range(2):
                src = fields[f].at[:, 3, :, 7 - j] if side == 0 else fields[f].at[:, 0, :, j]
                pltpu.make_async_remote_copy(
                    src,
                    halo.at[b, f, j],
                    side_send.at[side],
                    side_recv,
                    device_id=(target, side),
                    device_id_type=MESH,
                ).start()

    @pl.when(has_high)
    def _():
        to_layer(0, s + 1)

    @pl.when(has_low)
    def _():
        to_layer(1, s - 1)

    for f in range(3):
        for j in range(2):
            t, i = edge_row(b, j)
            pltpu.make_async_copy(
                fields[f].at[:, t, :, i], extra.at[f, j, mine], local_sem.at[1]
            ).start()
        for c in range(8):
            pltpu.make_async_copy(
                fields[f].at[:, mine, c], main.at[f, mine, :, :, c], local_sem.at[0]
            ).start()

    for t in tables:
        t.wait()
    next_to = jnp.where(b == 0, jnp.where(has_low, s - 1, s), jnp.where(has_high, s + 1, s))
    at_wall = ((b == 0) & (s == 0)) | ((b == 1) & (s == last))

    def slots_of(table, row):
        held = [table[k, row] for k in range(4)]
        return [
            jnp.where(held[1] == p, 1, jnp.where(held[2] == p, 2, jnp.where(held[3] == p, 3, 0)))
            for p in range(4)
        ]

    slot_here = slots_of(prior, s)
    slot_next = slots_of(prior, next_to)
    place_mine = [revised[2 * b + k, s] for k in range(2)]
    place_theirs = [revised[2 * ob + k, s] for k in range(2)]
    lane = lax.broadcasted_iota(jnp.int32, (8, 128), 1)
    lane_block = [lane < 32, lane < 64, lane < 96]

    def activity(row):
        a = [RATE * flags[p, row].astype(F32) for p in range(4)]
        low = jnp.where(lane_block[0], a[0], a[1])
        high = jnp.where(lane_block[2], a[2], a[3])
        return jnp.where(lane_block[1], low, high)

    active_here = activity(s)
    active_next = activity(next_to)

    def place(t, i):
        return jnp.where(b == 1, t, 1 - t), jnp.where(b == 1, i, 7 - i)

    def keep(u, planes, f):
        for r in range(4):
            first[f, u, r] = planes[r]

    def gather_extra(j):
        for f in range(3):
            keep(j, chunk_swap([extra[f, j, slot_here[p]] for p in range(4)], lane_block), f)

    def gather(t, i):
        tile, row = place(t, i)
        for f in range(3):
            planes = [main[f, slot_here[p], tile, row] for p in range(4)]
            keep(2 + 8 * t + i, chunk_swap(planes, lane_block), f)

    def gather_halo(j):
        for f in range(3):
            planes = chunk_swap(
                [halo[slot_next[p] // 2, f, j, slot_next[p] % 2] for p in range(4)], lane_block
            )
            keep(18 + j, [jnp.where(at_wall, first[f, 17, r], planes[r]) for r in range(4)], f)

    def rows(src, u):
        return [[src[f, u, r] for r in range(4)] for f in range(3)]

    def step_one(u):
        active = jnp.where(u == 18, active_next, active_here)
        new = advance(rows(first, u), rows(first, u - 1), rows(first, u + 1), active)
        for f in range(3):
            for r in range(4):
                second[f, u, r] = new[f][r]

    def step_two(u):
        new = advance(rows(second, u), rows(second, u - 1), rows(second, u + 1), active_here)
        for f in range(3):
            planes = chunk_swap(new[f], lane_block)
            for p in range(4):
                final[f, p, u - 2] = planes[p]

    def deal(t, i):
        tile, row = place(t, i)
        for f in range(3):
            for k in range(2):
                leaving[f, k, tile, row] = final[f, place_theirs[k], 8 * t + i]
                outs[f][k, 2 * b + tile, row] = final[f, place_mine[k], 8 * t + i]

    def back(f, t, h):
        tile, row = jnp.where(b == 1, t, 1 - t), jnp.where(b == 1, 4 * h, 4 - 4 * h)
        return pltpu.make_async_remote_copy(
            leaving.at[f, :, tile, pl.ds(row, 4)],
            outs[f].at[:, 2 * b + tile, pl.ds(row, 4)],
            back_send.at[2 * t + h, f],
            back_recv.at[2 * t + h, f],
            device_id=(s, ob),
            device_id_type=MESH,
        )

    def side_copy(side, ref):
        return pltpu.make_async_remote_copy(
            ref, ref, side_send.at[side], side_recv, device_id=(s, ob), device_id_type=MESH
        )

    pltpu.make_async_copy(main.at[:, mine], main.at[:, mine], local_sem.at[0]).wait()
    pltpu.make_async_copy(extra.at[:, :, mine], extra.at[:, :, mine], local_sem.at[1]).wait()
    other_core(extra.at[:, :, mine], extra.at[:, :, theirs], 1).wait_recv()
    other_core(main.at[:, mine], main.at[:, theirs], 0).wait_recv()
    def gather_tile(t, carry):
        for i in range(8):
            gather(t, i)
        return carry

    lax.fori_loop(0, 2, gather_tile, 0)
    for j in range(2):
        gather_extra(j)

    @pl.when(jnp.logical_not(at_wall))
    def _():
        side_copy(0, halo).wait_recv()

    for j in range(2):
        gather_halo(j)
    def step_rows(n, carry):
        for i in range(6):
            step_one(1 + 6 * n + i)
        return carry

    lax.fori_loop(0, 3, step_rows, 0)
    for f in range(3):
        for r in range(4):
            second[f, 18, r] = jnp.where(at_wall, second[f, 17, r], second[f, 18, r])

    def finish(n, carry):
        t, h = n // 2, n % 2
        for i in range(4):
            step_two(2 + 4 * n + i)
        for i in range(4):
            deal(t, 4 * h + i)
        for f in range(3):
            back(f, t, h).start()
        return carry

    lax.fori_loop(0, 4, finish, 0)

    other_core(main.at[:, mine], main.at[:, theirs], 0).wait_send()
    other_core(extra.at[:, :, mine], extra.at[:, :, theirs], 1).wait_send()

    @pl.when(has_high)
    def _():
        side_copy(0, halo.at[b]).wait_send()

    @pl.when(has_low)
    def _():
        side_copy(1, halo.at[b]).wait_send()

    for n in range(4):
        for f in range(3):
            back(f, n // 2, n % 2).wait()


def deliver(p_in, u_in, h_in, p_out, u_out, h_out, sem):
    pairs = ((p_in, p_out), (u_in, u_out), (h_in, h_out))
    for f, (src, dst) in enumerate(pairs):
        for c in range(8):
            pltpu.make_async_copy(src.at[:, :, :, c], dst.at[:, :, c], sem.at[f]).start()
    for f, (src, dst) in enumerate(pairs):
        pltpu.make_async_copy(src, dst, sem.at[f]).wait()


def body(slabs, p, u, h, prior, revised, flags):
    tiles = [a.reshape(2, 4, 8, 8, 128).transpose(0, 1, 3, 2, 4) for a in (p, u, h)]
    block = jax.ShapeDtypeStruct((2, 4, 8, 8, 128), F32)
    anywhere = pl.BlockSpec(memory_space=pl.ANY)
    hbm = pl.BlockSpec(memory_space=pltpu.HBM)
    vmem = pl.BlockSpec(memory_space=pltpu.VMEM)
    dma = pltpu.SemaphoreType.DMA
    table = pltpu.SMEM((4, slabs), jnp.int32)
    done = pl.pallas_call(
        functools.partial(kernel, slabs),
        out_shape=(block,) * 3,
        in_specs=[hbm] * 6,
        out_specs=(vmem,) * 3,
        scratch_shapes=[
            pltpu.VMEM((3, 4, 2, 8, 8, 128), F32),
            pltpu.VMEM((3, 2, 4, 8, 128), F32),
            pltpu.VMEM((2, 3, 2, 2, 8, 128), F32),
            pltpu.VMEM((3, 20, 4, 8, 128), F32),
            pltpu.VMEM((3, 20, 4, 8, 128), F32),
            pltpu.VMEM((3, 4, 16, 8, 128), F32),
            pltpu.VMEM((3, 2, 2, 8, 8, 128), F32),
            table,
            table,
            table,
            dma((3,)),
            dma((2,)),
            dma((2,)),
            dma((2,)),
            dma((2,)),
            dma,
            dma((4, 3)),
            dma((4, 3)),
        ],
        compiler_params=pltpu.CompilerParams(
            collective_id=0, has_side_effects=True, vmem_limit_bytes=16 << 20
        ),
        name="sweeps",
    )(*(pltpu.with_memory_space_constraint(a, pltpu.HBM) for a in (*tiles, prior.T, revised.T, flags.T)))
    placed = pl.pallas_call(
        deliver,
        out_shape=(block,) * 3,
        in_specs=[anywhere] * 3,
        out_specs=(anywhere,) * 3,
        scratch_shapes=[dma((3,))],
        compiler_params=pltpu.CompilerParams(vmem_limit_bytes=4 << 20),
        name="deliver",
    )(*done)
    return tuple(a.transpose(0, 1, 3, 2, 4).reshape(1, 2, 32, 1024) for a in placed)


def solution(mesh):
    blocks = P("slab", "bal", None, None)
    return jax.shard_map(
        functools.partial(body, mesh.shape["slab"]),
        mesh=mesh,
        in_specs=(blocks,) * 3 + (P(),) * 3,
        out_specs=(blocks,) * 3,
        check_vma=False,
    )
```

```python
import functools

import jax
import jax.numpy as jnp
from jax import lax
from jax.experimental import pallas as pl
from jax.experimental.pallas import tpu as pltpu
from jax.sharding import PartitionSpec as P

RATE = 0.1
ANISO = 0.05
COUPLE = 0.5
DIFF_SOLUTE = 0.08
DIFF_HEAT = 0.15
TINY = 0.0001

MESH = pl.DeviceIdType.MESH
F32 = jnp.float32


def chunk_swap(planes, lane_block):
    turned = [planes[0]] + [pltpu.roll(planes[p], 32 * p, 1) for p in (1, 2, 3)]
    out = []
    for k in range(4):
        pick = [turned[(j - k) % 4] for j in range(4)]
        low = jnp.where(lane_block[0], pick[0], pick[1])
        high = jnp.where(lane_block[2], pick[2], pick[3])
        both = jnp.where(lane_block[1], low, high)
        out.append(both if k == 0 else pltpu.roll(both, 128 - 32 * k, 1))
    return out


def advance(center, below, above, active):
    def total(f, r):
        plane = center[f]
        y_upper = plane[r + 1] if r < 3 else pltpu.roll(plane[0], 7, 0)
        y_lower = plane[r - 1] if r > 0 else pltpu.roll(plane[3], 1, 0)
        z_upper, z_lower = pltpu.roll(plane[r], 127, 1), pltpu.roll(plane[r], 1, 1)
        around = ((above[f][r] + below[f][r]) + (y_upper + y_lower)) + (z_upper + z_lower)
        return around, y_upper - y_lower, z_upper - z_lower

    out = [[], [], []]
    for r in range(4):
        phase, solute, heat = center[0][r], center[1][r], center[2][r]
        around, dy, dz = total(0, r)
        dx = above[0][r] - below[0][r]
        qx, qy, qz = dx * dx, dy * dy, dz * dz
        slope_sq = qx + qy + qz
        quartic = qx * qx + qy * qy + qz * qz
        ratio = quartic / (slope_sq * slope_sq + 16.0 * TINY)
        aniso = (1.0 - 3.0 * ANISO) + 4.0 * ANISO * ratio
        well = 1.0 - phase * phase
        forcing = well * (phase - (COUPLE * well) * (solute + heat))
        change = active * (aniso * aniso * (around - 6.0 * phase) + forcing)
        half = 0.5 * change
        out[0].append(phase + change)
        for f, rate, here in ((1, DIFF_SOLUTE, solute), (2, DIFF_HEAT, heat)):
            out[f].append(((1.0 - 6.0 * rate) * here + rate * total(f, r)[0]) + half)
    return out


def kernel(
    slabs,
    p_in,
    u_in,
    h_in,
    prior_in,
    revised_in,
    flags_in,
    p_out,
    u_out,
    h_out,
    main_p,
    main_u,
    main_h,
    extra_p,
    extra_u,
    extra_h,
    halo,
    first,
    second,
    final,
    leaving,
    prior,
    revised,
    flags,
    table_sem,
    local_sem,
    chip_send,
    chip_recv,
    side_send,
    side_recv,
    back_send,
    back_recv,
):
    fields = (p_in, u_in, h_in)
    outs = (p_out, u_out, h_out)
    main = (main_p, main_u, main_h)
    extra = (extra_p, extra_u, extra_h)
    s = lax.axis_index("slab")
    b = lax.axis_index("bal")
    ob = 1 - b
    last = slabs - 1
    has_low, has_high = s > 0, s < last
    barrier = pltpu.get_barrier_semaphore()

    pl.semaphore_signal(barrier, inc=1, device_id=(s, ob), device_id_type=MESH)

    @pl.when((b == 0) & has_low)
    def _():
        for k in range(2):
            pl.semaphore_signal(barrier, inc=1, device_id=(s - 1, k), device_id_type=MESH)

    @pl.when((b == 1) & has_high)
    def _():
        for k in range(2):
            pl.semaphore_signal(barrier, inc=1, device_id=(s + 1, k), device_id_type=MESH)

    tables = [
        pltpu.make_async_copy(src, dst, table_sem.at[i])
        for i, (src, dst) in enumerate(
            ((prior_in, prior), (revised_in, revised), (flags_in, flags))
        )
    ]
    for t in tables:
        t.start()
    pl.semaphore_wait(barrier, 1 + jnp.where(has_low, 1, 0) + jnp.where(has_high, 1, 0))

    def other_core(src, dst, i):
        return pltpu.make_async_remote_copy(
            src, dst, chip_send.at[i], chip_recv.at[i], device_id=(s, ob), device_id_type=MESH
        )

    mine = pl.ds(2 * b, 2)
    theirs = pl.ds(2 * ob, 2)

    def edge_row(core, j):
        return 2 - core, jnp.where(core == 1, 6 + j, 1 - j)

    for f in range(3):
        for j in range(2):
            t, i = edge_row(ob, j)
            other_core(fields[f].at[:, t, :, i], extra[f].at[j, mine], 3 + f).start()
        for c in range(8):
            other_core(fields[f].at[:, theirs, c], main[f].at[mine, :, :, c], f).start()

    def to_layer(side, target):
        for f in range(3):
            for j in range(2):
                src = fields[f].at[:, 3, :, 7 - j] if side == 0 else fields[f].at[:, 0, :, j]
                pltpu.make_async_remote_copy(
                    src,
                    halo.at[b, f, j],
                    side_send.at[side],
                    side_recv,
                    device_id=(target, side),
                    device_id_type=MESH,
                ).start()

    @pl.when(has_high)
    def _():
        to_layer(0, s + 1)

    @pl.when(has_low)
    def _():
        to_layer(1, s - 1)

    for f in range(3):
        for j in range(2):
            t, i = edge_row(b, j)
            pltpu.make_async_copy(
                fields[f].at[:, t, :, i], extra[f].at[j, mine], local_sem.at[3 + f]
            ).start()
        for c in range(8):
            pltpu.make_async_copy(
                fields[f].at[:, mine, c], main[f].at[mine, :, :, c], local_sem.at[f]
            ).start()

    for t in tables:
        t.wait()
    next_to = jnp.where(b == 0, jnp.where(has_low, s - 1, s), jnp.where(has_high, s + 1, s))
    at_wall = ((b == 0) & (s == 0)) | ((b == 1) & (s == last))

    def slots_of(table, row):
        held = [table[k, row] for k in range(4)]
        return [
            jnp.where(held[1] == p, 1, jnp.where(held[2] == p, 2, jnp.where(held[3] == p, 3, 0)))
            for p in range(4)
        ]

    slot_here = slots_of(prior, s)
    slot_next = slots_of(prior, next_to)
    place_mine = [revised[2 * b + k, s] for k in range(2)]
    place_theirs = [revised[2 * ob + k, s] for k in range(2)]
    lane = lax.broadcasted_iota(jnp.int32, (8, 128), 1)
    lane_block = [lane < 32, lane < 64, lane < 96]

    def activity(row):
        a = [RATE * flags[p, row].astype(F32) for p in range(4)]
        low = jnp.where(lane_block[0], a[0], a[1])
        high = jnp.where(lane_block[2], a[2], a[3])
        return jnp.where(lane_block[1], low, high)

    active_here = activity(s)
    active_next = activity(next_to)

    def place(t, i):
        return jnp.where(b == 1, t, 1 - t), jnp.where(b == 1, i, 7 - i)

    def keep(u, planes, f):
        for r in range(4):
            first[f, u, r] = planes[r]

    def gather_extra(f, j):
        keep(j, chunk_swap([extra[f][j, slot_here[p]] for p in range(4)], lane_block), f)

    def gather(f, t, i):
        tile, row = place(t, i)
        planes = [main[f][slot_here[p], tile, row] for p in range(4)]
        keep(2 + 8 * t + i, chunk_swap(planes, lane_block), f)

    def gather_halo(j):
        for f in range(3):
            planes = chunk_swap(
                [halo[slot_next[p] // 2, f, j, slot_next[p] % 2] for p in range(4)], lane_block
            )
            keep(18 + j, [jnp.where(at_wall, first[f, 17, r], planes[r]) for r in range(4)], f)

    def rows(src, u):
        return [[src[f, u, r] for r in range(4)] for f in range(3)]

    def step_one(u):
        active = jnp.where(u == 18, active_next, active_here)
        new = advance(rows(first, u), rows(first, u - 1), rows(first, u + 1), active)
        for f in range(3):
            for r in range(4):
                second[f, u, r] = new[f][r]

    def step_two(u):
        new = advance(rows(second, u), rows(second, u - 1), rows(second, u + 1), active_here)
        for f in range(3):
            planes = chunk_swap(new[f], lane_block)
            for p in range(4):
                final[f, p, u - 2] = planes[p]

    def deal(t, i):
        tile, row = place(t, i)
        for f in range(3):
            for k in range(2):
                leaving[f, k, tile, row] = final[f, place_theirs[k], 8 * t + i]
                outs[f][k, 2 * b + tile, row] = final[f, place_mine[k], 8 * t + i]

    def back(f, t, h):
        tile, row = jnp.where(b == 1, t, 1 - t), jnp.where(b == 1, 4 * h, 4 - 4 * h)
        return pltpu.make_async_remote_copy(
            leaving.at[f, :, tile, pl.ds(row, 4)],
            outs[f].at[:, 2 * b + tile, pl.ds(row, 4)],
            back_send.at[2 * t + h, f],
            back_recv.at[2 * t + h, f],
            device_id=(s, ob),
            device_id_type=MESH,
        )

    def side_copy(side, ref):
        return pltpu.make_async_remote_copy(
            ref, ref, side_send.at[side], side_recv, device_id=(s, ob), device_id_type=MESH
        )

    for f in range(3):
        own = main[f].at[mine]
        own_edge = extra[f].at[:, mine]
        pltpu.make_async_copy(own, own, local_sem.at[f]).wait()
        pltpu.make_async_copy(own_edge, own_edge, local_sem.at[3 + f]).wait()
        other_core(own_edge, extra[f].at[:, theirs], 3 + f).wait_recv()
        other_core(own, main[f].at[theirs], f).wait_recv()

        for t in range(2):
            gather_extra(f, t)
            for i in range(8):
                gather(f, t, i)

    @pl.when(jnp.logical_not(at_wall))
    def _():
        side_copy(0, halo).wait_recv()

    for j in range(2):
        gather_halo(j)

    def step_rows(n, carry):
        for i in range(9):
            step_one(1 + 9 * n + i)
        return carry

    lax.fori_loop(0, 2, step_rows, 0)
    for f in range(3):
        for r in range(4):
            second[f, 18, r] = jnp.where(at_wall, second[f, 17, r], second[f, 18, r])

    def finish(n, carry):
        t, h = n // 2, n % 2
        for i in range(4):
            step_two(2 + 4 * n + i)
        for i in range(4):
            deal(t, 4 * h + i)
        for f in range(3):
            back(f, t, h).start()
        return carry

    lax.fori_loop(0, 4, finish, 0)

    for f in range(3):
        other_core(main[f].at[mine], main[f].at[theirs], f).wait_send()
        other_core(extra[f].at[:, mine], extra[f].at[:, theirs], 3 + f).wait_send()

    @pl.when(has_high)
    def _():
        side_copy(0, halo.at[b]).wait_send()

    @pl.when(has_low)
    def _():
        side_copy(1, halo.at[b]).wait_send()

    for n in range(4):
        for f in range(3):
            back(f, n // 2, n % 2).wait()


def deliver(p_in, u_in, h_in, p_out, u_out, h_out, sem):
    pairs = ((p_in, p_out), (u_in, u_out), (h_in, h_out))
    for f, (src, dst) in enumerate(pairs):
        for c in range(8):
            pltpu.make_async_copy(src.at[:, :, :, c], dst.at[:, :, c], sem.at[f]).start()
    for f, (src, dst) in enumerate(pairs):
        pltpu.make_async_copy(src, dst, sem.at[f]).wait()


def body(slabs, p, u, h, prior, revised, flags):
    tiles = [a.reshape(2, 4, 8, 8, 128).transpose(0, 1, 3, 2, 4) for a in (p, u, h)]
    block = jax.ShapeDtypeStruct((2, 4, 8, 8, 128), F32)
    anywhere = pl.BlockSpec(memory_space=pl.ANY)
    hbm = pl.BlockSpec(memory_space=pltpu.HBM)
    vmem = pl.BlockSpec(memory_space=pltpu.VMEM)
    dma = pltpu.SemaphoreType.DMA
    table = pltpu.SMEM((4, slabs), jnp.int32)
    done = pl.pallas_call(
        functools.partial(kernel, slabs),
        out_shape=(block,) * 3,
        in_specs=[hbm] * 6,
        out_specs=(vmem,) * 3,
        scratch_shapes=[
            *[pltpu.VMEM((4, 2, 8, 8, 128), F32)] * 3,
            *[pltpu.VMEM((2, 4, 8, 128), F32)] * 3,
            pltpu.VMEM((2, 3, 2, 2, 8, 128), F32),
            pltpu.VMEM((3, 20, 4, 8, 128), F32),
            pltpu.VMEM((3, 20, 4, 8, 128), F32),
            pltpu.VMEM((3, 4, 16, 8, 128), F32),
            pltpu.VMEM((3, 2, 2, 8, 8, 128), F32),
            table,
            table,
            table,
            dma((3,)),
            dma((6,)),
            dma((6,)),
            dma((6,)),
            dma((2,)),
            dma,
            dma((4, 3)),
            dma((4, 3)),
        ],
        compiler_params=pltpu.CompilerParams(
            collective_id=0, has_side_effects=True, vmem_limit_bytes=16 << 20
        ),
        name="sweeps",
    )(*(pltpu.with_memory_space_constraint(a, pltpu.HBM) for a in (*tiles, prior.T, revised.T, flags.T)))
    placed = pl.pallas_call(
        deliver,
        out_shape=(block,) * 3,
        in_specs=[anywhere] * 3,
        out_specs=(anywhere,) * 3,
        scratch_shapes=[dma((3,))],
        compiler_params=pltpu.CompilerParams(vmem_limit_bytes=4 << 20),
        name="deliver",
    )(*done)
    return tuple(a.transpose(0, 1, 3, 2, 4).reshape(1, 2, 32, 1024) for a in placed)


def solution(mesh):
    blocks = P("slab", "bal", None, None)
    return jax.shard_map(
        functools.partial(body, mesh.shape["slab"]),
        mesh=mesh,
        in_specs=(blocks,) * 3 + (P(),) * 3,
        out_specs=(blocks,) * 3,
        check_vma=False,
    )
```
